32 devices in a mesh: groups: 2 (over y), dp: 4 (over z), ctx: 4 (over x, core).
Axes of the slice: x: 2, y: 2, z: 4, core: 2. Of those that a mesh axis runs over, the one named last changes fastest.
Arguments:
- queries: bfloat16 [8, 1024, 2048], P(('groups', 'dp'), 'ctx'), parts along dimension 0, may hold values from -480 to 480
- keys: bfloat16 [8, 1024, 256], P(('groups', 'dp'), 'ctx'), parts along dimension 0, may hold values from -4.1 to 4.1
- values: bfloat16 [8, 1024, 256], P(('groups', 'dp'), 'ctx'), parts along dimension 0, may hold values from -6 to 6
- grad_out: bfloat16 [8, 1024, 2048], P(('groups', 'dp'), 'ctx'), parts along dimension 0, may hold values from -6 to 6
- sinks: float32 [32], replicated, may hold values from 0 to 6
- doc_ids: int32 [8, 1024], P(('groups', 'dp')), parts along dimension 0, may hold values from 0 to 1, never falling along the last dimension, each value on 1 to 768 neighbouring positions
- swap_flags: int32 [8, 4, 16], P(('groups', 'dp'), 'ctx'), parts along dimension 0, may hold values from 0 to 1, as said below
Outputs:
- attn_out: bfloat16 [8, 1024, 2048], P(('groups', 'dp'), 'ctx'), parts along dimension 0
- grad_queries: bfloat16 [8, 1024, 2048], P(('groups', 'dp'), 'ctx'), parts along dimension 0
- grad_keys: bfloat16 [8, 1024, 256], P(('groups', 'dp'), 'ctx'), parts along dimension 0
- grad_values: bfloat16 [8, 1024, 256], P(('groups', 'dp'), 'ctx'), parts along dimension 0
The draws below stay inside these ranges and needn't reach their ends.
There are 2 independent parts, one for each index of `groups`. The reference program is written for one: setup_inputs(seed, part) draws one part's arguments, and reference() takes and returns one part's arrays. A program takes and returns all parts, laid end to end along the dimension named above; an argument that names none is the same for every part. Nothing has to cross between parts.
Inputs may be any that keep to these rules, and one draw needn't show every extreme that they name: `doc_ids`: each of the 2 responses of a pack covers between 256 and 768 neighbouring positions. swap_flags of rank i and run c equal those of its partner rank (i + 2) mod 4 and run c; each device has at most 1 ones, and some device has exactly 1.
All inputs are finite; a program needn't handle non-finite values.
Results may differ from the reference program's by a relative error of at most 0.019.
Values may be sent and summed in bfloat16 or wider, within the bound.
No kernel may reach another device: no remote copies, remote signals or barrier semaphores. Data moves between devices by JAX's collectives and lax.ppermute only.
A program may use at most 64 MiB of HBM per device.

```python
import math
import jax
import jax.numpy as jnp
import numpy as np
from jax import lax

QUERY_HEADS = 32
KEY_VALUE_HEADS = 4
HEAD_SIZE = 64
WINDOW = 128
BLK = 16
CAP = 1
SEQS = 2
BLOCKS = 16
ROWS = 256
BATCH_PACKS = 4
STRETCHES = 4
PACK_TOKENS = 1024
DOC_MOST = 768


def draw_queries(key, part):
    leading_key = jax.random.fold_in(jax.random.fold_in(key, 11), 0)
    start_offset = jnp.clip(jax.random.normal(leading_key, (BATCH_PACKS, PACK_TOKENS, QUERY_HEADS * HEAD_SIZE), jnp.float32), -4.0, 4.0)
    return start_offset.astype(jnp.bfloat16)


def draw_keys(key, part):
    leading_key = jax.random.fold_in(jax.random.fold_in(key, 23), 0)
    start_offset = jnp.clip(jax.random.normal(leading_key, (BATCH_PACKS, PACK_TOKENS, KEY_VALUE_HEADS * HEAD_SIZE), jnp.float32), -4.0, 4.0)
    return start_offset.astype(jnp.bfloat16)


def draw_swap_flags(key, part):
    count_key, order_key, pair_key, run_key = jax.random.split(jax.random.fold_in(key, 37), 4)
    half_packs = BATCH_PACKS // 2
    counts = jax.random.randint(count_key, (half_packs, STRETCHES), 0, CAP + 1)
    full_pair = jax.random.randint(pair_key, (), 0, half_packs)
    full_run = jax.random.randint(run_key, (), 0, STRETCHES)
    counts = counts.at[full_pair, full_run].set(CAP)
    noise_bits = jax.random.randint(order_key, (half_packs, STRETCHES, BLOCKS), 0, 1 << 20)
    distinct = noise_bits * BLOCKS + jnp.arange(BLOCKS, dtype=jnp.int32)[None, None, :]
    ranking = jnp.argsort(jnp.argsort(distinct, axis=-1), axis=-1)
    lower_half = (ranking < counts[:, :, None]).astype(jnp.int32)
    return jnp.concatenate([lower_half, lower_half], axis=0)


def shard_levels(rng, shape, cuts, least, largest):
    gain, own = 1.0, jax.random.fold_in(rng, 6)
    for position, blocks in cuts:
        steps = jnp.exp(jax.random.uniform(jax.random.fold_in(own, position), (blocks,), jnp.float32, least / len(cuts), largest / len(cuts)))
        gain = gain * jnp.repeat(steps, shape[position] // blocks).reshape([-1 if axis == position else 1 for axis in range(len(shape))])
    return gain


def split_up(amount, total, limit, slope):
    weights = [(1 << 20) // math.isqrt(standing ** slope) + 1 for standing in range(2, amount + 1)]
    surplus, holding = total - limit - (amount - 1), [1] * (amount - 1)
    while surplus > 0:
        candidates = [i for i in range(amount - 1) if holding[i] < limit]
        whole, left = sum([weights[i] for i in candidates]), surplus
        for i in candidates:
            extra = min(limit - holding[i], max(1, left * weights[i] // whole), surplus)
            holding[i] = holding[i] + extra
            surplus = surplus - extra
    return np.array([limit] + holding)


def ragged(key, count, total, bound, slope):
    if count == 2:
        one = jax.random.randint(key, (), max(1, total - bound), min(bound, total - 1) + 1)
        return jnp.stack([one, total - one])
    tallies = jnp.asarray(split_up(count, total, bound, slope), jnp.int32)
    couples = (count - 1) // 2
    donor, taker = tallies[1:1 + 2 * couples:2], tallies[2:2 + 2 * couples:2]
    slack = jnp.minimum(donor - 1, bound - taker)
    moved = jax.random.randint(jax.random.fold_in(key, 1), (couples,), 0, 1 << 20) % (slack + 1)
    tallies = tallies.at[1:1 + 2 * couples:2].set(donor - moved).at[2:2 + 2 * couples:2].set(taker + moved)
    return tallies[jax.random.permutation(jax.random.fold_in(key, 2), count)]


def centred(rng, dims, scale, most, shards=(), held_as=jnp.bfloat16):
    drawn = jax.random.normal(rng, dims, jnp.float32) * scale
    if len(shards) > 0:
        drawn = shard_levels(rng, dims, shards, -0.22, 0.18) * drawn
    return jnp.clip(drawn, min=-most, max=most).astype(held_as)


def setup_inputs(seed: int = 0, part: int = 0) -> dict:
    arg_keys = jax.random.split(jax.random.key(seed), 8)
    own_keys = jax.random.split(jax.random.fold_in(arg_keys[7], part), 8)
    queries = draw_queries(jax.random.fold_in(jax.random.fold_in(arg_keys[7], part), 71), part)
    keys = draw_keys(jax.random.fold_in(jax.random.fold_in(arg_keys[7], part), 71), part)
    values = centred(own_keys[2], (BATCH_PACKS, PACK_TOKENS, KEY_VALUE_HEADS * HEAD_SIZE), 1.0, 6.0, ((0, 4), (1, 4)))
    grad_out = centred(own_keys[3], (BATCH_PACKS, PACK_TOKENS, QUERY_HEADS * HEAD_SIZE), 1.0, 6.0, ((0, 4), (1, 4)))
    sinks = jnp.clip(jax.random.uniform(arg_keys[4], (QUERY_HEADS,), jnp.float32, 0.0, 6.0), 0.0, 6.0)
    doc_ids = jax.vmap(lambda own: jnp.searchsorted(jnp.cumsum(ragged(own, SEQS, PACK_TOKENS, DOC_MOST, 1)), jnp.arange(PACK_TOKENS), side="right"))(jax.random.split(own_keys[5], BATCH_PACKS)).reshape((BATCH_PACKS, PACK_TOKENS)).astype(jnp.int32)
    swap_flags = draw_swap_flags(jax.random.fold_in(jax.random.fold_in(arg_keys[7], part), 71), part)
    return {"queries": queries, "keys": keys, "values": values, "grad_out": grad_out, "sinks": sinks, "doc_ids": doc_ids, "swap_flags": swap_flags}


def attend(query_matrix, key_matrix, value_matrix, gradient_rows, sink_scores_raw, query_docs, key_docs, query_pos, key_pos):
    query_count = query_matrix.shape[0]
    key_count = key_matrix.shape[0]
    heads_per_group = QUERY_HEADS // KEY_VALUE_HEADS
    score_scale = 1.0 / math.sqrt(HEAD_SIZE)
    queries_float = query_matrix.astype(jnp.float32).reshape(query_count, KEY_VALUE_HEADS, heads_per_group, HEAD_SIZE)
    gradients_float = gradient_rows.astype(jnp.float32).reshape(query_count, KEY_VALUE_HEADS, heads_per_group, HEAD_SIZE)
    keys_float = key_matrix.astype(jnp.float32).reshape(key_count, KEY_VALUE_HEADS, HEAD_SIZE)
    values_float = value_matrix.astype(jnp.float32).reshape(key_count, KEY_VALUE_HEADS, HEAD_SIZE)
    scores = jnp.einsum('rkgd,lkd->kgrl', queries_float, keys_float) * score_scale
    distance = query_pos[:, None] - key_pos[None, :]
    allowed = (query_docs[:, None] == key_docs[None, :]) & (distance >= 0) & (distance < WINDOW)
    sink_fraction = sink_scores_raw.astype(jnp.float32).reshape(KEY_VALUE_HEADS, heads_per_group)[:, :, None]
    masked = jnp.where(allowed, scores, jnp.float32(-1e+30))
    top = jnp.maximum(lax.optimization_barrier(jnp.max(masked, axis=-1)), sink_fraction)
    expo = jnp.where(allowed, jnp.exp(masked - top[..., None]), jnp.float32(0.0))
    total = jnp.exp(sink_fraction - top) + lax.optimization_barrier(jnp.sum(expo, axis=-1))
    probs = expo / total[..., None]
    probs_b = lax.optimization_barrier(probs.astype(jnp.bfloat16)).astype(jnp.float32)
    out_f = jnp.einsum('kgrl,lkd->rkgd', probs_b, values_float)
    output_blocks = lax.optimization_barrier(out_f.astype(jnp.bfloat16))
    row_dot = jnp.einsum('rkgd,rkgd->kgr', gradients_float, output_blocks.astype(jnp.float32))
    dprobs = jnp.einsum('rkgd,lkd->kgrl', gradients_float, values_float)
    dscores = probs * (dprobs - row_dot[..., None])
    dscores_b = lax.optimization_barrier(dscores.astype(jnp.bfloat16)).astype(jnp.float32)
    query_gradient = (jnp.einsum('kgrl,lkd->rkgd', dscores_b, keys_float) * score_scale).astype(jnp.bfloat16)
    key_gradient = jnp.einsum('kgrl,rkgd->lkd', dscores_b, queries_float) * score_scale
    value_gradient = jnp.einsum('kgrl,rkgd->lkd', probs_b, gradients_float)
    return (output_blocks.reshape(query_count, QUERY_HEADS * HEAD_SIZE), query_gradient.reshape(query_count, QUERY_HEADS * HEAD_SIZE), key_gradient.reshape(key_count, KEY_VALUE_HEADS * HEAD_SIZE), value_gradient.reshape(key_count, KEY_VALUE_HEADS * HEAD_SIZE))

def reference(queries, keys, values, grad_out, sinks, doc_ids, swap_flags):

    def trade_blocks(array):
        width = array.shape[-1]
        shaped = array.reshape(BATCH_PACKS, STRETCHES, BLOCKS, BLK, width)
        partnered = jnp.roll(shaped, BATCH_PACKS // 2, axis=0)
        traded = jnp.where(swap_flags[:, :, :, None, None] == 1, partnered, shaped)
        return traded.reshape(BATCH_PACKS, PACK_TOKENS, width)
    packed_q = trade_blocks(queries)
    packed_k = trade_blocks(keys)
    packed_v = trade_blocks(values)
    packed_g = trade_blocks(grad_out)
    key_span_width = KEY_VALUE_HEADS * HEAD_SIZE
    span = ROWS + WINDOW

    def one_pack(inputs):
        pack_q, pack_k, pack_v, pack_g, pack_docs = inputs
        keys_pad = jnp.concatenate([jnp.zeros((WINDOW, key_span_width), pack_k.dtype), pack_k], axis=0)
        values_pad = jnp.concatenate([jnp.zeros((WINDOW, key_span_width), pack_v.dtype), pack_v], axis=0)
        docs_pad = jnp.concatenate([jnp.full((WINDOW,), -1, jnp.int32), pack_docs.astype(jnp.int32)], axis=0)

        def run_step(running, run_index):
            grad_k_acc, grad_v_acc = running
            offset = (run_index * ROWS).astype(jnp.int32)
            query_matrix = lax.dynamic_slice_in_dim(pack_q, offset, ROWS, 0)
            gradient_rows = lax.dynamic_slice_in_dim(pack_g, offset, ROWS, 0)
            key_matrix = lax.dynamic_slice_in_dim(keys_pad, offset, span, 0)
            value_matrix = lax.dynamic_slice_in_dim(values_pad, offset, span, 0)
            query_docs = lax.dynamic_slice_in_dim(pack_docs.astype(jnp.int32), offset, ROWS, 0)
            key_docs = lax.dynamic_slice_in_dim(docs_pad, offset, span, 0)
            query_pos = offset + jnp.arange(ROWS, dtype=jnp.int32)
            key_pos = offset - WINDOW + jnp.arange(span, dtype=jnp.int32)
            output_blocks, query_gradient, key_gradient, value_gradient = attend(query_matrix, key_matrix, value_matrix, gradient_rows, sinks, query_docs, key_docs, query_pos, key_pos)
            old_k = lax.dynamic_slice_in_dim(grad_k_acc, offset, span, 0)
            old_v = lax.dynamic_slice_in_dim(grad_v_acc, offset, span, 0)
            grad_k_acc = lax.dynamic_update_slice_in_dim(grad_k_acc, old_k + key_gradient, offset, 0)
            grad_v_acc = lax.dynamic_update_slice_in_dim(grad_v_acc, old_v + value_gradient, offset, 0)
            return ((grad_k_acc, grad_v_acc), (output_blocks, query_gradient))
        start_state = (jnp.zeros((PACK_TOKENS + WINDOW, key_span_width), jnp.float32), jnp.zeros((PACK_TOKENS + WINDOW, key_span_width), jnp.float32))
        (grad_k_acc, grad_v_acc), (outs_b, grads_q) = lax.scan(run_step, start_state, jnp.arange(STRETCHES, dtype=jnp.int32))
        return (outs_b.reshape(PACK_TOKENS, QUERY_HEADS * HEAD_SIZE), grads_q.reshape(PACK_TOKENS, QUERY_HEADS * HEAD_SIZE), grad_k_acc[WINDOW:].astype(jnp.bfloat16), grad_v_acc[WINDOW:].astype(jnp.bfloat16))
    packed_out, packed_dq, packed_dk, packed_dv = lax.map(one_pack, (packed_q, packed_k, packed_v, packed_g, doc_ids))
    return (trade_blocks(packed_out), trade_blocks(packed_dq), trade_blocks(packed_dk), trade_blocks(packed_dv))
```

```python
import functools
import math

import jax
import jax.numpy as jnp
from jax import lax
from jax.experimental import pallas as pl
from jax.experimental.pallas import tpu as pltpu
from jax.sharding import PartitionSpec as P

QUERY_HEADS = 32
KEY_VALUE_HEADS = 4
HEAD_SIZE = 64
WINDOW = 128
TILE = 128
SPAN = TILE + WINDOW
PAIR = 2 * HEAD_SIZE
GROUP = QUERY_HEADS // KEY_VALUE_HEADS
PAIRS = GROUP // 2
HALVES = KEY_VALUE_HEADS // 2
NEG = -1e30
F32 = jnp.float32
BF16 = jnp.bfloat16


def mm(a, b):
    return lax.dot_general(a, b, (((1,), (0,)), ((), ())), preferred_element_type=F32)


def mm_nt(a, b):
    return lax.dot_general(a, b, (((1,), (1,)), ((), ())), preferred_element_type=F32)


def low_lanes(rows, lanes=PAIR):
    return lax.broadcasted_iota(jnp.int32, (rows, lanes), 1) < HEAD_SIZE


def spread_head(pair, odd):
    wide = pair.astype(F32)
    low = low_lanes(wide.shape[0])
    if odd:
        high = jnp.where(low, 0.0, wide)
        return pltpu.roll(high, HEAD_SIZE, 1), high
    lower = jnp.where(low, wide, 0.0)
    return lower, pltpu.roll(lower, HEAD_SIZE, 1)


def head_operands(k_pair, v_pair, odd):
    rows = k_pair.shape[0]
    scale = 1.0 / math.sqrt(HEAD_SIZE)
    k_lo, k_hi = spread_head(k_pair, odd)
    v_lo, v_hi = spread_head(v_pair, odd)
    low = low_lanes(rows)
    ones_lo = jnp.where(low, 1.0, 0.0)
    ones_hi = jnp.where(low, 0.0, 1.0)
    return (
        (k_lo * scale).astype(BF16),
        (k_hi * scale).astype(BF16),
        jnp.concatenate([v_lo, ones_lo], axis=1).astype(BF16),
        jnp.concatenate([v_hi, ones_hi], axis=1).astype(BF16),
    )


def attend_pair(q, g, operands, bias, sink_even, sink_odd):
    k_lo, k_hi, v_lo, v_hi = operands
    rows = q.shape[0]
    low = low_lanes(rows)
    expos, tops = [], []
    for k_half, sink in ((k_lo, sink_even), (k_hi, sink_odd)):
        scores = mm_nt(q, k_half) + bias
        top = jnp.maximum(jnp.max(scores, axis=1, keepdims=True), sink)
        expos.append(jnp.exp(scores - top))
        tops.append(jnp.exp(sink - top))
    rounded = [expo.astype(BF16) for expo in expos]
    mixed = mm(rounded[0], v_lo) + mm(rounded[1], v_hi)
    inverse = 1.0 / (mixed[:, PAIR:] + jnp.where(low, tops[0], tops[1]))
    out = (mixed[:, :PAIR] * inverse).astype(BF16)
    weighted = (g.astype(F32) * inverse).astype(BF16)
    product = weighted.astype(F32) * out.astype(F32)
    dots = (
        jnp.sum(jnp.where(low, product, 0.0), axis=1, keepdims=True),
        jnp.sum(jnp.where(low, 0.0, product), axis=1, keepdims=True),
    )
    deltas = []
    for expo, dot, v_half in ((expos[0], dots[0], v_lo), (expos[1], dots[1], v_hi)):
        deltas.append((expo * (mm_nt(weighted, v_half[:, :PAIR]) - dot)).astype(BF16))
    dq = (mm(deltas[0], k_lo) + mm(deltas[1], k_hi)).astype(BF16)
    return out, dq, weighted, rounded, deltas


def key_sums(stacked, both):
    turned = jnp.transpose(stacked)
    return mm(
        jnp.concatenate([turned[:HEAD_SIZE], turned[HEAD_SIZE:]], axis=1),
        jnp.concatenate(both, axis=0),
    )


def tile_work(q_ref, g_ref, sinks_ref, k_ext, v_ext, bias, out_ref, dq_ref, half):
    dk_parts, dv_parts = [], []
    for odd in range(2):
        operands = head_operands(k_ext, v_ext, odd)
        dk = dv = None
        for pair in range(PAIRS):
            head = odd * GROUP + 2 * pair
            lanes = slice(head * HEAD_SIZE, (head + 2) * HEAD_SIZE)
            index = half * (2 * GROUP) + head
            q = q_ref[:, lanes]
            out, dq, weighted, rounded, deltas = attend_pair(
                q, g_ref[:, lanes], operands, bias, sinks_ref[index], sinks_ref[index + 1]
            )
            out_ref[:, lanes] = out
            dq_ref[:, lanes] = dq
            dk_one = key_sums(q, deltas)
            dv_one = key_sums(weighted, rounded)
            dk = dk_one if dk is None else dk + dk_one
            dv = dv_one if dv is None else dv + dv_one
        dk_parts.append(dk)
        dv_parts.append(dv)
    scale = 1.0 / math.sqrt(HEAD_SIZE)
    return (
        jnp.transpose(jnp.concatenate(dk_parts, axis=0)) * scale,
        jnp.transpose(jnp.concatenate(dv_parts, axis=0)),
    )


def flagged(flags_ref, count):
    amount = flags_ref[0]
    number = jnp.int32(0)
    for block in range(1, count):
        amount = amount + flags_ref[block]
        number = number + flags_ref[block] * block
    return amount, number


def pick_kernel(blocks, first_tail, flags_ref, q_ref, g_ref, k_ref, v_ref, kt_ref, vt_ref, qg_ref, kv_ref, tail_ref):
    amount, number = flagged(flags_ref, blocks)
    wide = q_ref.shape[1]
    qg_ref[:, :wide] = q_ref[...]
    qg_ref[:, wide:] = g_ref[...]
    kv_ref[:, :PAIR] = k_ref[...]
    kv_ref[:, PAIR:] = v_ref[...]
    tail_ref[:WINDOW, :PAIR] = kt_ref[...]
    tail_ref[:WINDOW, PAIR:] = vt_ref[...]
    mark = jnp.where(amount * number >= first_tail, number - first_tail + 1, 0)
    tail_ref[WINDOW:, :] = jnp.full((tail_ref.shape[0] - WINDOW, 2 * PAIR), mark.astype(F32)).astype(BF16)


def fill_own(own_ref, blocks, block_rows, flags_ref, incoming_ref, kv_scr, base):
    amount, number = flagged(flags_ref, blocks)
    own_k, own_v = own_ref
    rows = own_k.shape[0]
    kv_scr[base : base + rows, :PAIR] = own_k[...]
    kv_scr[base : base + rows, PAIR:] = own_v[...]

    @pl.when(amount > 0)
    def _():
        start = pl.multiple_of(base + number * block_rows, block_rows)
        kv_scr[pl.ds(start, block_rows), :] = incoming_ref[...]

    return amount, number


def fill_halo(tail_ref, cross_ref, block_rows, kv_scr):
    kv_scr[:WINDOW, :] = tail_ref[:WINDOW, :]
    mark = jnp.max(tail_ref[WINDOW:, :].astype(F32)).astype(jnp.int32)

    @pl.when(mark > 0)
    def _():
        start = pl.multiple_of((mark - 1) * block_rows, block_rows)
        kv_scr[pl.ds(start, block_rows), :] = cross_ref[...]

    return mark


def late_kernel(blocks, block_rows, flags_ref, sinks_ref, q_ref, g_ref, k_ref, v_ref, kv_ref, bias_ref, out_ref, dq_ref, dkv_ref, kv_scr):
    fill_own((k_ref, v_ref), blocks, block_rows, flags_ref, kv_ref, kv_scr, 0)
    kv = kv_scr[...]
    dk, dv = tile_work(q_ref, g_ref, sinks_ref, kv[:, :PAIR], kv[:, PAIR:], bias_ref[...], out_ref, dq_ref, pl.program_id(0))
    dkv_ref[:, :PAIR] = dk
    dkv_ref[:, PAIR:] = dv


def swap_kernel(blocks, block_rows, flags_ref, sinks_ref, qg_ref, k_ref, v_ref, kv_ref, tail_ref, cross_ref, bias_ref, oq_ref, dkv_ref, kv_scr):
    half = pl.program_id(0)
    _, number = fill_own((k_ref, v_ref), blocks, block_rows, flags_ref, kv_ref, kv_scr, WINDOW)
    fill_halo(tail_ref, cross_ref, block_rows, kv_scr)
    limit = kv_scr.shape[0] - SPAN
    start = pl.multiple_of(jnp.minimum(number * block_rows, limit), block_rows)
    kv = kv_scr[pl.ds(start, SPAN), :]
    wide = qg_ref.shape[1] // 2
    bias = bias_ref[...]
    scale = 1.0 / math.sqrt(HEAD_SIZE)
    dk_parts, dv_parts = [], []
    for odd in range(2):
        operands = head_operands(kv[:, :PAIR], kv[:, PAIR:], odd)
        first = odd * GROUP
        spots = [slice((first + 2 * pair) * HEAD_SIZE, (first + 2 * pair + 2) * HEAD_SIZE) for pair in range(PAIRS)]
        q = jnp.concatenate([qg_ref[:, spot] for spot in spots], axis=0)
        g = jnp.concatenate([qg_ref[:, wide + spot.start : wide + spot.stop] for spot in spots], axis=0)
        base = half * (2 * GROUP) + first
        sinks = [
            jnp.concatenate(
                [jnp.full((block_rows, 1), sinks_ref[base + 2 * pair + side], F32) for pair in range(PAIRS)], axis=0
            )
            for side in range(2)
        ]
        out, dq, weighted, rounded, deltas = attend_pair(q, g, operands, bias, sinks[0], sinks[1])
        for pair, spot in enumerate(spots):
            rows = slice(pair * block_rows, (pair + 1) * block_rows)
            oq_ref[:, spot] = out[rows]
            oq_ref[:, wide + spot.start : wide + spot.stop] = dq[rows]
        q_t = jnp.transpose(q.astype(F32)).astype(BF16)
        w_t = jnp.transpose(weighted.astype(F32)).astype(BF16)
        dk_parts.append(mm(q_t[:HEAD_SIZE], deltas[0]) + mm(q_t[HEAD_SIZE:], deltas[1]))
        dv_parts.append(mm(w_t[:HEAD_SIZE], rounded[0]) + mm(w_t[HEAD_SIZE:], rounded[1]))
    dkv_ref[:, :PAIR] = jnp.transpose(jnp.concatenate(dk_parts, axis=0)) * scale
    dkv_ref[:, PAIR:] = jnp.transpose(jnp.concatenate(dv_parts, axis=0))


def early_kernel(
    blocks, block_rows, flags_ref, sinks_ref, q_ref, g_ref, k_ref, v_ref, kv_ref, tail_ref, cross_ref, bias_ref,
    late_ref, swap_ref, out_in, dq_in, out_ref, dq_ref, own_ref, back_ref, cross_back_ref, trade_ref, kv_scr, dkv_scr,
):
    amount, number = fill_own((k_ref, v_ref), blocks, block_rows, flags_ref, kv_ref, kv_scr, WINDOW)
    mark = fill_halo(tail_ref, cross_ref, block_rows, kv_scr)
    kv = kv_scr[:SPAN, :]
    dk, dv = tile_work(q_ref, g_ref, sinks_ref, kv[:, :PAIR], kv[:, PAIR:], bias_ref[...], out_ref, dq_ref, pl.program_id(0))
    own_rows = late_ref.shape[0]
    dkv_scr[:WINDOW, :PAIR] = dk[:WINDOW]
    dkv_scr[:WINDOW, PAIR:] = dv[:WINDOW]
    dkv_scr[WINDOW:SPAN, :PAIR] = dk[WINDOW:] + late_ref[:TILE, :PAIR]
    dkv_scr[WINDOW:SPAN, PAIR:] = dv[WINDOW:] + late_ref[:TILE, PAIR:]
    dkv_scr[SPAN:, :] = late_ref[TILE:, :]

    @pl.when(amount > 0)
    def _():
        limit = dkv_scr.shape[0] - SPAN
        start = pl.multiple_of(jnp.minimum(number * block_rows, limit), block_rows)
        dkv_scr[pl.ds(start, SPAN), :] = dkv_scr[pl.ds(start, SPAN), :] + swap_ref[...]

    own_ref[...] = dkv_scr[WINDOW:, :]
    back_ref[...] = dkv_scr[:WINDOW, :].astype(BF16)
    spot = pl.multiple_of(WINDOW + number * block_rows, block_rows)
    trade_ref[...] = dkv_scr[pl.ds(spot, block_rows), :].astype(BF16)
    cross = pl.multiple_of(jnp.maximum(mark - 1, 0) * block_rows, block_rows)
    cross_back_ref[...] = dkv_scr[pl.ds(cross, block_rows), :].astype(BF16)


def finish_kernel(
    blocks, block_rows, flags_ref, oq_ref, own_ref, back_ref, cross_ref, trade_ref, out_in, dq_in,
    out_ref, dq_ref, dk_ref, dv_ref, sem,
):
    amount, number = flagged(flags_ref, blocks)
    start = pl.multiple_of(number * block_rows, block_rows)
    width = oq_ref.shape[1] // (2 * HALVES)
    copies = []
    for half in range(HALVES):
        for side, target in enumerate((out_ref, dq_ref)):
            lanes = (2 * half + side) * width
            copies.append(
                pltpu.make_async_copy(
                    oq_ref.at[:, pl.ds(lanes, width)],
                    target.at[pl.ds(start, block_rows), pl.ds(half * width, width)],
                    sem.at[2 * half + side],
                )
            )

    @pl.when(amount > 0)
    def _():
        for copy in copies:
            copy.start()

    rows = own_ref.shape[0]
    tail = rows - WINDOW
    for half in range(HALVES):
        for side, target in enumerate((dk_ref, dv_ref)):
            source = slice((2 * half + side) * PAIR, (2 * half + side + 1) * PAIR)
            lanes = slice(half * PAIR, (half + 1) * PAIR)
            target[:tail, lanes] = own_ref[:tail, source].astype(BF16)
            target[tail:, lanes] = (own_ref[tail:, source] + back_ref[:, source].astype(F32)).astype(BF16)

    @pl.when(amount > 0)
    def _():
        tail_part = jnp.where(start >= tail, 1.0, 0.0)
        for half in range(HALVES):
            for side, target in enumerate((dk_ref, dv_ref)):
                source = slice((2 * half + side) * PAIR, (2 * half + side + 1) * PAIR)
                lanes = slice(half * PAIR, (half + 1) * PAIR)
                total = trade_ref[:, source].astype(F32) + tail_part * cross_ref[:, source].astype(F32)
                target[pl.ds(start, block_rows), lanes] = total.astype(BF16)
        for copy in copies:
            copy.wait()


def shards(queries, keys, values, grad_out, sinks, doc_ids, swap_flags):
    rows, query_width = queries.shape[1:]
    key_width = keys.shape[2]
    flags = swap_flags[0, 0]
    blocks = flags.shape[0]
    block_rows = rows // blocks
    first_tail = (rows - WINDOW) // block_rows
    late_tile = rows // TILE - 1
    q, k, v, g = queries[0], keys[0], values[0], grad_out[0]
    wide = query_width // HALVES
    packs = lax.axis_size("dp")
    runs = lax.axis_size("ctx")
    partner = [(rank, (rank + packs // 2) % packs) for rank in range(packs)]
    forward = [(run, run + 1) for run in range(runs - 1)]
    across = [
        (rank * runs + run, (rank + packs // 2) % packs * runs + run + 1)
        for rank in range(packs)
        for run in range(runs - 1)
    ]

    def number_of(flags_ref):
        return sum(flags_ref[block] * block for block in range(1, blocks))

    def spec(shape, index):
        return pl.BlockSpec(shape, index)

    half_specs = lambda height, width, row=0: spec((height, width), lambda s, *_: (row, s))
    params = dict(compiler_params=pltpu.CompilerParams(dimension_semantics=("arbitrary",)))
    any_spec = pl.BlockSpec(memory_space=pl.ANY)

    qg_out, kv_out, tail_out = pl.pallas_call(
        functools.partial(pick_kernel, blocks, first_tail),
        grid_spec=pltpu.PrefetchScalarGridSpec(
            num_scalar_prefetch=1,
            grid=(HALVES,),
            in_specs=[
                spec((block_rows, wide), lambda s, f: (number_of(f), s)),
                spec((block_rows, wide), lambda s, f: (number_of(f), s)),
                spec((block_rows, PAIR), lambda s, f: (number_of(f), s)),
                spec((block_rows, PAIR), lambda s, f: (number_of(f), s)),
                half_specs(WINDOW, PAIR, rows // WINDOW - 1),
                half_specs(WINDOW, PAIR, rows // WINDOW - 1),
            ],
            out_specs=[
                half_specs(block_rows, 2 * wide),
                half_specs(block_rows, 2 * PAIR),
                half_specs(WINDOW + block_rows, 2 * PAIR),
            ],
        ),
        out_shape=[
            jax.ShapeDtypeStruct((block_rows, 2 * query_width), BF16),
            jax.ShapeDtypeStruct((block_rows, 2 * key_width), BF16),
            jax.ShapeDtypeStruct((WINDOW + block_rows, 2 * key_width), BF16),
        ],
        cost_estimate=pl.CostEstimate(flops=0, bytes_accessed=1 << 20, transcendentals=0),
        name="pick",
        **params,
    )(flags, q, g, k, v, k, v)

    kv_in = lax.ppermute(kv_out, "dp", partner)
    tail_in = lax.ppermute(tail_out, "ctx", forward)
    cross_in = lax.ppermute(kv_out, ("dp", "ctx"), across)
    qg_in = lax.ppermute(qg_out, "dp", partner)

    run = lax.axis_index("ctx")
    pack_docs = doc_ids[0]
    docs_pad = jnp.concatenate([jnp.full((WINDOW,), -1, jnp.int32), pack_docs])
    docs = lax.dynamic_slice_in_dim(docs_pad, run * rows, rows + WINDOW, 0)
    number = jnp.sum(flags * jnp.arange(blocks, dtype=jnp.int32))
    amount = jnp.sum(flags)

    def bias_of(query_docs, query_spots, key_docs, key_spots, keep):
        distance = query_spots[:, None] - key_spots[None, :]
        seen = (query_docs[:, None] == key_docs[None, :]) & (distance >= 0) & (distance < WINDOW)
        return jnp.where(seen & keep[:, None], F32(0.0), F32(NEG))

    spots = jnp.arange(rows + WINDOW, dtype=jnp.int32)
    kept = jnp.repeat(flags == 0, block_rows)

    def tile_bias(tile):
        low = tile * TILE
        return bias_of(
            docs[WINDOW + low : WINDOW + low + TILE],
            spots[WINDOW + low : WINDOW + low + TILE],
            docs[low : low + SPAN],
            spots[low : low + SPAN],
            kept[low : low + TILE],
        )

    bias_late = tile_bias(late_tile)
    bias_early = tile_bias(0)
    start = jnp.minimum(number * block_rows, rows + WINDOW - SPAN)
    swap_rows = jnp.tile(lax.dynamic_slice_in_dim(docs, WINDOW + number * block_rows, block_rows, 0), PAIRS)
    swap_spots = jnp.tile(WINDOW + number * block_rows + jnp.arange(block_rows, dtype=jnp.int32), PAIRS)
    bias_swap = bias_of(
        swap_rows,
        swap_spots,
        lax.dynamic_slice_in_dim(docs, start, SPAN, 0),
        start + jnp.arange(SPAN, dtype=jnp.int32),
        jnp.broadcast_to(amount > 0, (PAIRS * block_rows,)),
    )

    tile_cost = pl.CostEstimate(flops=int(6e9), bytes_accessed=2 << 20, transcendentals=1 << 20)
    whole_bias = spec((TILE, SPAN), lambda s, *_: (0, 0))
    scalars = dict(num_scalar_prefetch=2, grid=(HALVES,))

    out_late, dq_late, dkv_late = pl.pallas_call(
        functools.partial(late_kernel, blocks, block_rows),
        grid_spec=pltpu.PrefetchScalarGridSpec(
            **scalars,
            in_specs=[
                half_specs(TILE, wide, late_tile),
                half_specs(TILE, wide, late_tile),
                half_specs(rows, PAIR),
                half_specs(rows, PAIR),
                half_specs(block_rows, 2 * PAIR),
                whole_bias,
            ],
            out_specs=[
                half_specs(TILE, wide, late_tile),
                half_specs(TILE, wide, late_tile),
                half_specs(rows, 2 * PAIR),
            ],
            scratch_shapes=[pltpu.VMEM((rows, 2 * PAIR), BF16)],
        ),
        out_shape=[
            jax.ShapeDtypeStruct((rows, query_width), BF16),
            jax.ShapeDtypeStruct((rows, query_width), BF16),
            jax.ShapeDtypeStruct((rows, 2 * key_width), F32),
        ],
        cost_estimate=tile_cost,
        name="late",
        **params,
    )(flags, sinks, q, g, k, v, kv_in, bias_late)

    qg_in, dkv_late = lax.optimization_barrier((qg_in, dkv_late))

    oq_out, dkv_swap = pl.pallas_call(
        functools.partial(swap_kernel, blocks, block_rows),
        grid_spec=pltpu.PrefetchScalarGridSpec(
            **scalars,
            in_specs=[
                half_specs(block_rows, 2 * wide),
                half_specs(rows, PAIR),
                half_specs(rows, PAIR),
                half_specs(block_rows, 2 * PAIR),
                half_specs(WINDOW + block_rows, 2 * PAIR),
                half_specs(block_rows, 2 * PAIR),
                spec((PAIRS * block_rows, SPAN), lambda s, *_: (0, 0)),
            ],
            out_specs=[half_specs(block_rows, 2 * wide), half_specs(SPAN, 2 * PAIR)],
            scratch_shapes=[pltpu.VMEM((rows + WINDOW, 2 * PAIR), BF16)],
        ),
        out_shape=[
            jax.ShapeDtypeStruct((block_rows, 2 * query_width), BF16),
            jax.ShapeDtypeStruct((SPAN, 2 * key_width), F32),
        ],
        cost_estimate=pl.CostEstimate(flops=int(5e8), bytes_accessed=1 << 20, transcendentals=1 << 18),
        name="swap",
        **params,
    )(flags, sinks, qg_in, k, v, kv_in, tail_in, cross_in, bias_swap)

    oq_in = lax.ppermute(oq_out, "dp", partner)

    out_all, dq_all, dkv_own, back_out, cross_out, trade_out = pl.pallas_call(
        functools.partial(early_kernel, blocks, block_rows),
        grid_spec=pltpu.PrefetchScalarGridSpec(
            **scalars,
            in_specs=[
                half_specs(TILE, wide),
                half_specs(TILE, wide),
                half_specs(rows, PAIR),
                half_specs(rows, PAIR),
                half_specs(block_rows, 2 * PAIR),
                half_specs(WINDOW + block_rows, 2 * PAIR),
                half_specs(block_rows, 2 * PAIR),
                whole_bias,
                half_specs(rows, 2 * PAIR),
                half_specs(SPAN, 2 * PAIR),
                any_spec,
                any_spec,
            ],
            out_specs=[
                half_specs(TILE, wide),
                half_specs(TILE, wide),
                half_specs(rows, 2 * PAIR),
                half_specs(WINDOW, 2 * PAIR),
                half_specs(block_rows, 2 * PAIR),
                half_specs(block_rows, 2 * PAIR),
            ],
            scratch_shapes=[
                pltpu.VMEM((rows + WINDOW, 2 * PAIR), BF16),
                pltpu.VMEM((rows + WINDOW, 2 * PAIR), F32),
            ],
        ),
        out_shape=[
            jax.ShapeDtypeStruct((rows, query_width), BF16),
            jax.ShapeDtypeStruct((rows, query_width), BF16),
            jax.ShapeDtypeStruct((rows, 2 * key_width), F32),
            jax.ShapeDtypeStruct((WINDOW, 2 * key_width), BF16),
            jax.ShapeDtypeStruct((block_rows, 2 * key_width), BF16),
            jax.ShapeDtypeStruct((block_rows, 2 * key_width), BF16),
        ],
        input_output_aliases={12: 0, 13: 1},
        cost_estimate=tile_cost,
        name="early",
        **params,
    )(flags, sinks, q, g, k, v, kv_in, tail_in, cross_in, bias_early, dkv_late, dkv_swap, out_late, dq_late)

    back_in = lax.ppermute(back_out, "ctx", [(target, source) for source, target in forward])
    cross_back = lax.ppermute(cross_out, ("dp", "ctx"), [(target, source) for source, target in across])
    trade_in = lax.ppermute(trade_out, "dp", partner)

    vmem = pl.BlockSpec(memory_space=pltpu.VMEM)
    final = pl.pallas_call(
        functools.partial(finish_kernel, blocks, block_rows),
        in_specs=[pl.BlockSpec(memory_space=pltpu.SMEM)] + [vmem] * 5 + [any_spec] * 2,
        out_specs=[any_spec, any_spec, vmem, vmem],
        out_shape=[
            jax.ShapeDtypeStruct((rows, query_width), BF16),
            jax.ShapeDtypeStruct((rows, query_width), BF16),
            jax.ShapeDtypeStruct((rows, key_width), BF16),
            jax.ShapeDtypeStruct((rows, key_width), BF16),
        ],
        scratch_shapes=[pltpu.SemaphoreType.DMA((2 * HALVES,))],
        input_output_aliases={6: 0, 7: 1},
        cost_estimate=pl.CostEstimate(flops=0, bytes_accessed=1 << 20, transcendentals=0),
        name="finish",
    )(flags, oq_in, dkv_own, back_in, cross_back, trade_in, out_all, dq_all)
    return tuple(array[None] for array in final)


def solution(mesh):
    blocks = P(("groups", "dp"), "ctx", None)
    in_specs = (blocks, blocks, blocks, blocks, P(), P(("groups", "dp"), None), blocks)
    out_specs = (blocks, blocks, blocks, blocks)
    return jax.shard_map(shards, mesh=mesh, in_specs=in_specs, out_specs=out_specs, check_vma=False)
```

```python
import functools
import math

import jax
import jax.numpy as jnp
from jax import lax
from jax.experimental import pallas as pl
from jax.experimental.pallas import tpu as pltpu
from jax.sharding import PartitionSpec as P

QUERY_HEADS = 32
KEY_VALUE_HEADS = 4
HEAD_SIZE = 64
WINDOW = 128
TILE = 128
SPAN = TILE + WINDOW
PAIR = 2 * HEAD_SIZE
GROUP = QUERY_HEADS // KEY_VALUE_HEADS
PAIRS = GROUP // 2
NEG = -1e30
SCALE = 1.0 / math.sqrt(HEAD_SIZE)
F32 = jnp.float32
BF16 = jnp.bfloat16


def mm(a, b):
    return lax.dot_general(a, b, (((1,), (0,)), ((), ())), preferred_element_type=F32)


def mm_nt(a, b):
    return lax.dot_general(a, b, (((1,), (1,)), ((), ())), preferred_element_type=F32)


def low_lanes(rows):
    return lax.broadcasted_iota(jnp.int32, (rows, PAIR), 1) < HEAD_SIZE


def spread_head(pair, odd):
    wide = pair.astype(F32)
    low = low_lanes(wide.shape[0])
    if odd:
        high = jnp.where(low, 0.0, wide)
        return pltpu.roll(high, HEAD_SIZE, 1), high
    lower = jnp.where(low, wide, 0.0)
    return lower, pltpu.roll(lower, HEAD_SIZE, 1)


def head_operands(kv, head):
    width = kv.shape[1] // 2
    lanes = slice(head // 2 * PAIR, (head // 2 + 1) * PAIR)
    keys = spread_head(kv[:, lanes], head % 2)
    values = spread_head(kv[:, width + lanes.start : width + lanes.stop], head % 2)
    low = low_lanes(kv.shape[0])
    ones = (jnp.where(low, 1.0, 0.0), jnp.where(low, 0.0, 1.0))
    return (
        jnp.concatenate([part * SCALE for part in keys], axis=0).astype(BF16),
        jnp.concatenate([jnp.concatenate(both, axis=1) for both in zip(values, ones)], axis=0).astype(BF16),
    )


def score_stage(q, operands, bias, sinks):
    found = []
    span = bias.shape[1]
    products = mm_nt(q, operands[0])
    for side, sink in enumerate(sinks):
        scores = products[:, side * span : (side + 1) * span] + bias
        found.append((scores, jnp.maximum(jnp.max(scores, axis=1, keepdims=True), sink)))
    return found


def output_stage(g, operands, found, sinks):
    low = low_lanes(g.shape[0])
    repeats = found[0][0].shape[1] // PAIR
    expos = [jnp.exp(scores - jnp.concatenate([top] * repeats, axis=1)) for scores, top in found]
    rounded = jnp.concatenate([expo.astype(BF16) for expo in expos], axis=1)
    rest = jnp.where(low, jnp.exp(sinks[0] - found[0][1]), jnp.exp(sinks[1] - found[1][1]))
    mixed = mm(rounded, operands[1])
    inverse = 1.0 / (mixed[:, PAIR:] + rest)
    out = (mixed[:, :PAIR] * inverse).astype(BF16)
    weighted = (g.astype(F32) * inverse).astype(BF16)
    product = weighted.astype(F32) * out.astype(F32)
    dots = (
        jnp.sum(jnp.where(low, product, 0.0), axis=1, keepdims=True),
        jnp.sum(jnp.where(low, 0.0, product), axis=1, keepdims=True),
    )
    return out, weighted, expos, rounded, dots


def gradient_stage(q, operands, weighted, expos, rounded, dots):
    span = expos[0].shape[1]
    products = mm_nt(weighted, operands[1][:, :PAIR])
    deltas = jnp.concatenate(
        [
            (expo * (products[:, side * span : (side + 1) * span] - dot)).astype(BF16)
            for side, (expo, dot) in enumerate(zip(expos, dots))
        ],
        axis=1,
    )
    return mm(deltas, operands[0]).astype(BF16), key_sums(q, deltas), key_sums(weighted, rounded)


def key_sums(stacked, both):
    span = both.shape[1] // 2
    turned = jnp.transpose(stacked)
    if stacked.shape[0] % PAIR == 0:
        return mm(
            jnp.concatenate([turned[:HEAD_SIZE], turned[HEAD_SIZE:]], axis=1),
            jnp.concatenate([both[:, :span], both[:, span:]], axis=0),
        )
    return mm(turned[:HEAD_SIZE], both[:, :span]) + mm(turned[HEAD_SIZE:], both[:, span:])


def attend_heads(q_of, g_of, sinks_ref, kv, bias, finish, skew):
    rows = bias.shape[0]
    bias = jnp.concatenate([bias] * PAIRS, axis=0)
    first, second = {}, {}
    dk, dv = [], []
    for step in range(KEY_VALUE_HEADS + 2 * skew):
        head = step
        if head < KEY_VALUE_HEADS:
            spots = [slice((head * PAIRS + pair) * PAIR, (head * PAIRS + pair + 1) * PAIR) for pair in range(PAIRS)]
            q = jnp.concatenate([q_of(spot) for spot in spots], axis=0)
            sinks = [
                jnp.concatenate(
                    [jnp.full((rows, PAIR), sinks_ref[head * GROUP + 2 * pair + side], F32) for pair in range(PAIRS)],
                    axis=0,
                )
                for side in range(2)
            ]
            operands = head_operands(kv, head)
            first[head] = (spots, q, operands, sinks, score_stage(q, operands, bias, sinks))
        head = step - skew
        if 0 <= head < KEY_VALUE_HEADS:
            spots, q, operands, sinks, found = first.pop(head)
            g = jnp.concatenate([g_of(spot) for spot in spots], axis=0)
            second[head] = (spots, q, operands) + output_stage(g, operands, found, sinks)
        head = step - 2 * skew
        if 0 <= head < KEY_VALUE_HEADS:
            spots, q, operands, out, *rest = second.pop(head)
            dq, dk_one, dv_one = gradient_stage(q, operands, *rest)
            finish(head, spots, out, dq)
            dk.append(dk_one)
            dv.append(dv_one)
    turn = lambda parts: jnp.concatenate(
        [jnp.transpose(jnp.concatenate(parts[i : i + 2], axis=0)) for i in range(0, KEY_VALUE_HEADS, 2)], axis=1
    )
    return turn(dk) * SCALE, turn(dv)


def flagged(flags_ref):
    amount = flags_ref[0, 0, 0]
    number = jnp.int32(0)
    for block in range(1, flags_ref.shape[2]):
        amount = amount + flags_ref[0, 0, block]
        number = number + flags_ref[0, 0, block] * block
    return amount, number


def pick_kernel(block_rows, flags_ref, q_ref, g_ref, k_ref, v_ref, qg_ref, kv_ref, tail_ref, sem):
    rows, width = q_ref.shape
    key_width = k_ref.shape[1]
    amount, number = flagged(flags_ref)
    block = pl.ds(pl.multiple_of(number * block_rows, block_rows), block_rows)
    last = slice(rows - WINDOW, rows)
    copies = [
        pltpu.make_async_copy(k_ref.at[last, :], tail_ref.at[:WINDOW, :key_width], sem.at[0]),
        pltpu.make_async_copy(v_ref.at[last, :], tail_ref.at[:WINDOW, key_width:], sem.at[1]),
        pltpu.make_async_copy(k_ref.at[block, :], kv_ref.at[:, :key_width], sem.at[2]),
        pltpu.make_async_copy(v_ref.at[block, :], kv_ref.at[:, key_width:], sem.at[3]),
        pltpu.make_async_copy(q_ref.at[block, :], qg_ref.at[:, :width], sem.at[4]),
        pltpu.make_async_copy(g_ref.at[block, :], qg_ref.at[:, width:], sem.at[5]),
    ]
    for copy in copies:
        copy.start()
    first_tail = (rows - WINDOW) // block_rows
    mark = jnp.where(amount * number >= first_tail, number - first_tail + 1, 0)
    tail_ref[WINDOW:, :] = jnp.full((block_rows, 2 * key_width), mark.astype(F32)).astype(BF16)
    for copy in copies:
        copy.wait()


def fill_keys(block_rows, flags_ref, k_ref, v_ref, kv_ref, kv_scr, base):
    amount, number = flagged(flags_ref)
    rows, key_width = k_ref.shape
    kv_scr[base : base + rows, :key_width] = k_ref[...]
    kv_scr[base : base + rows, key_width:] = v_ref[...]

    @pl.when(amount > 0)
    def _():
        start = pl.multiple_of(base + number * block_rows, block_rows)
        kv_scr[pl.ds(start, block_rows), :] = kv_ref[...]

    return amount, number


def fill_halo(block_rows, tail_ref, cross_ref, kv_scr):
    kv_scr[:WINDOW, :] = tail_ref[:WINDOW, :]
    mark = jnp.max(tail_ref[WINDOW:, :].astype(F32)).astype(jnp.int32)

    @pl.when(mark > 0)
    def _():
        start = pl.multiple_of((mark - 1) * block_rows, block_rows)
        kv_scr[pl.ds(start, block_rows), :] = cross_ref[...]

    return mark


def doc_row(docs_ref, chunk):
    row = docs_ref[pl.ds(jnp.maximum(chunk, 0), 1), :].astype(F32)
    return jnp.where(chunk < 0, -1.0, row)


def doc_column(docs_ref, chunk):
    return jnp.transpose(jnp.broadcast_to(doc_row(docs_ref, chunk), (WINDOW, WINDOW)))


def tile_bias(block_rows, tile, rows, amount, number, docs_ref):
    chunk = lax.axis_index("ctx") * (rows // WINDOW) + tile
    column = doc_column(docs_ref, chunk)
    row = lax.broadcasted_iota(jnp.int32, (TILE, WINDOW), 0)
    lane = lax.broadcasted_iota(jnp.int32, (TILE, WINDOW), 1)
    block = row // block_rows + tile * (TILE // block_rows)
    kept = jnp.logical_or(block != number, amount == 0)
    behind = (column == doc_row(docs_ref, chunk - 1)) & (lane > row) & kept
    beside = (column == doc_row(docs_ref, chunk)) & (lane <= row) & kept
    return jnp.concatenate([jnp.where(behind, 0.0, NEG), jnp.where(beside, 0.0, NEG)], axis=1)


def tile_work(block_rows, tile, flags, sinks_ref, docs_ref, q_ref, g_ref, kv, out_ref, dq_ref, out_scr, dq_scr, sem):
    amount, number = flags
    here = slice(tile * TILE, (tile + 1) * TILE)
    bias = tile_bias(block_rows, tile, q_ref.shape[0], amount, number, docs_ref)
    copies = []

    def finish(head, spots, out, dq):
        for pair, spot in enumerate(spots):
            part = slice(pair * TILE, (pair + 1) * TILE)
            out_scr[:, spot] = out[part]
            dq_scr[:, spot] = dq[part]
        lanes = slice(spots[0].start, spots[-1].stop)
        for side, (source, target) in enumerate(((out_scr, out_ref), (dq_scr, dq_ref))):
            copy = pltpu.make_async_copy(source.at[:, lanes], target.at[here, lanes], sem.at[2 * head + side])
            copy.start()
            copies.append(copy)

    dk, dv = attend_heads(
        lambda spot: q_ref[here, spot], lambda spot: g_ref[here, spot], sinks_ref, kv, bias, finish, 1
    )
    return dk, dv, copies


def late_kernel(
    block_rows, flags_ref, sinks_ref, docs_ref, q_ref, g_ref, k_ref, v_ref, kv_ref,
    out_ref, dq_ref, dkv_ref, kv_scr, out_scr, dq_scr, sem,
):
    rows, key_width = k_ref.shape
    flags = fill_keys(block_rows, flags_ref, k_ref, v_ref, kv_ref, kv_scr, 0)
    dk, dv, copies = tile_work(
        block_rows, rows // TILE - 1, flags, sinks_ref, docs_ref, q_ref, g_ref, kv_scr[rows - SPAN :, :],
        out_ref, dq_ref, out_scr, dq_scr, sem,
    )
    dkv_ref[:, :key_width] = dk
    dkv_ref[:, key_width:] = dv
    for copy in copies:
        copy.wait()


def swap_kernel(
    block_rows, flags_ref, sinks_ref, docs_ref, qg_ref, k_ref, v_ref, kv_ref, tail_ref, cross_ref,
    oq_ref, dkv_ref, kv_scr, doc_scr,
):
    rows, key_width = k_ref.shape
    width = qg_ref.shape[1] // 2
    amount, number = fill_keys(block_rows, flags_ref, k_ref, v_ref, kv_ref, kv_scr, WINDOW)
    fill_halo(block_rows, tail_ref, cross_ref, kv_scr)
    chunk = lax.axis_index("ctx") * (rows // WINDOW)
    per = WINDOW // block_rows
    doc_scr[...] = doc_column(docs_ref, chunk + number // per)
    column = doc_scr[pl.ds(pl.multiple_of(number % per * block_rows, block_rows), block_rows), :]
    row = lax.broadcasted_iota(jnp.int32, (block_rows, WINDOW), 0) + (WINDOW + number * block_rows)
    lane = lax.broadcasted_iota(jnp.int32, (block_rows, WINDOW), 1)
    parts = []
    for part in range(rows // WINDOW + 1):
        distance = row - lane - part * WINDOW
        seen = (column == doc_row(docs_ref, chunk + part - 1)) & (distance >= 0) & (distance < WINDOW) & (amount > 0)
        parts.append(jnp.where(seen, 0.0, NEG))

    def finish(head, spots, out, dq):
        for pair, spot in enumerate(spots):
            part = slice(pair * block_rows, (pair + 1) * block_rows)
            oq_ref[:, spot] = out[part]
            oq_ref[:, width + spot.start : width + spot.stop] = dq[part]

    dk, dv = attend_heads(
        lambda spot: qg_ref[:, spot],
        lambda spot: qg_ref[:, width + spot.start : width + spot.stop],
        sinks_ref, kv_scr[...], jnp.concatenate(parts, axis=1), finish, 1,
    )
    dkv_ref[:, :key_width] = dk
    dkv_ref[:, key_width:] = dv


def early_kernel(
    block_rows, flags_ref, sinks_ref, docs_ref, q_ref, g_ref, k_ref, v_ref, kv_ref, tail_ref, cross_ref,
    late_ref, swap_ref, out_in, dq_in, out_ref, dq_ref, own_ref, back_ref, cross_back_ref, trade_ref,
    kv_scr, dkv_scr, out_scr, dq_scr, sem,
):
    rows, key_width = k_ref.shape
    flags = fill_keys(block_rows, flags_ref, k_ref, v_ref, kv_ref, kv_scr, WINDOW)
    mark = fill_halo(block_rows, tail_ref, cross_ref, kv_scr)
    dk, dv, copies = tile_work(
        block_rows, 0, flags, sinks_ref, docs_ref, q_ref, g_ref, kv_scr[:SPAN, :], out_ref, dq_ref, out_scr, dq_scr, sem
    )
    dkv = jnp.concatenate([dk, dv], axis=1) + swap_ref[:SPAN, :]
    late = late_ref.shape[0] - (rows + WINDOW - SPAN)
    dkv_scr[:WINDOW, :] = dkv[:WINDOW]
    dkv_scr[WINDOW:SPAN, :] = dkv[WINDOW:] + late_ref[:late, :]
    dkv_scr[SPAN:, :] = late_ref[late:, :] + swap_ref[SPAN:, :]
    own_ref[...] = dkv_scr[WINDOW:, :]
    back_ref[...] = dkv[:WINDOW].astype(BF16)
    spot = pl.multiple_of(WINDOW + flags[1] * block_rows, block_rows)
    trade_ref[...] = dkv_scr[pl.ds(spot, block_rows), :].astype(BF16)
    cross = pl.multiple_of(jnp.maximum(mark - 1, 0) * block_rows, block_rows)
    cross_back_ref[...] = dkv_scr[pl.ds(cross, block_rows), :].astype(BF16)
    for copy in copies:
        copy.wait()


def finish_kernel(
    block_rows, flags_ref, oq_ref, own_ref, back_ref, cross_ref, trade_ref, out_in, dq_in,
    out_ref, dq_ref, dk_ref, dv_ref, sem,
):
    amount, number = flagged(flags_ref)
    start = pl.multiple_of(number * block_rows, block_rows)
    width = oq_ref.shape[1] // 2
    copies = [
        pltpu.make_async_copy(
            oq_ref.at[:, side * width : (side + 1) * width], target.at[pl.ds(start, block_rows), :], sem.at[side]
        )
        for side, target in enumerate((out_ref, dq_ref))
    ]

    @pl.when(amount > 0)
    def _():
        for copy in copies:
            copy.start()

    rows, key_width = dk_ref.shape
    tail = rows - WINDOW
    for side, target in enumerate((dk_ref, dv_ref)):
        lanes = slice(side * key_width, (side + 1) * key_width)
        target[:tail, :] = own_ref[:tail, lanes].astype(BF16)
        target[tail:, :] = (own_ref[tail:, lanes] + back_ref[:, lanes].astype(F32)).astype(BF16)

    @pl.when(amount > 0)
    def _():
        tail_part = jnp.where(start >= tail, 1.0, 0.0)
        total = (trade_ref[...].astype(F32) + tail_part * cross_ref[...].astype(F32)).astype(BF16)
        dk_ref[pl.ds(start, block_rows), :] = total[:, :key_width]
        dv_ref[pl.ds(start, block_rows), :] = total[:, key_width:]
        for copy in copies:
            copy.wait()


def shards(queries, keys, values, grad_out, sinks, doc_ids, swap_flags):
    rows, width = queries.shape[1:]
    key_width = keys.shape[2]
    block_rows = rows // swap_flags.shape[2]
    q, k, v, g = queries[0], keys[0], values[0], grad_out[0]
    docs = doc_ids.reshape(doc_ids.shape[1] // WINDOW, WINDOW)
    packs = lax.axis_size("dp")
    runs = lax.axis_size("ctx")
    partner = [(rank, (rank + packs // 2) % packs) for rank in range(packs)]
    forward = [(run, (run + 1) % runs) for run in range(runs)]
    across = [
        (rank * runs + run, (rank + packs // 2) % packs * runs + (run + 1) % runs)
        for rank in range(packs)
        for run in range(runs)
    ]
    reverse = lambda pairs: [(target, source) for source, target in pairs]

    vmem = pl.BlockSpec(memory_space=pltpu.VMEM)
    smem = pl.BlockSpec(memory_space=pltpu.SMEM)
    anywhere = pl.BlockSpec(memory_space=pltpu.HBM)
    wide = jax.ShapeDtypeStruct((rows, width), BF16)

    def call(body, name, in_specs, out_specs, out_shape, scratch, cost, mib, aliases={}):
        return pl.pallas_call(
            functools.partial(body, block_rows),
            in_specs=in_specs,
            out_specs=out_specs,
            out_shape=out_shape,
            scratch_shapes=scratch,
            input_output_aliases=aliases,
            cost_estimate=pl.CostEstimate(flops=int(cost), bytes_accessed=1 << 20, transcendentals=0),
            compiler_params=pltpu.CompilerParams(vmem_limit_bytes=mib << 20),
            name=name,
        )

    def made(height, lanes, dtype=BF16):
        return jax.ShapeDtypeStruct((height, lanes), dtype)

    qg_out, kv_out, tail_out = call(
        pick_kernel, "pick", [smem] + [anywhere] * 4, [vmem] * 3,
        [made(block_rows, 2 * width), made(block_rows, 2 * key_width), made(WINDOW + block_rows, 2 * key_width)],
        [pltpu.SemaphoreType.DMA((6,))], 1e6, 4,
    )(swap_flags, q, g, k, v)

    kv_in = lax.ppermute(kv_out, "dp", partner)
    cross_in = lax.ppermute(kv_out, ("dp", "ctx"), across)
    tail_in = lax.ppermute(tail_out, "ctx", forward)
    qg_in = lax.ppermute(qg_out, "dp", partner)

    tile_scratch = [
        pltpu.VMEM((TILE, width), BF16),
        pltpu.VMEM((TILE, width), BF16),
        pltpu.SemaphoreType.DMA((2 * KEY_VALUE_HEADS,)),
    ]
    head = [smem, smem, vmem]
    out_late, dq_late, dkv_late = call(
        late_kernel, "late", head + [vmem] * 5, [anywhere, anywhere, vmem],
        [wide, wide, made(SPAN, 2 * key_width, F32)],
        [pltpu.VMEM((rows, 2 * key_width), BF16)] + tile_scratch, 6e9, 24,
    )(swap_flags, sinks, docs, q, g, k, v, kv_in)

    qg_in, dkv_late = lax.optimization_barrier((qg_in, dkv_late))

    oq_out, dkv_swap = call(
        swap_kernel, "swap", head + [vmem] * 6, [vmem, vmem],
        [made(block_rows, 2 * width), made(rows + WINDOW, 2 * key_width, F32)],
        [pltpu.VMEM((rows + WINDOW, 2 * key_width), BF16), pltpu.VMEM((WINDOW, WINDOW), F32)], 1e9, 16,
    )(swap_flags, sinks, docs, qg_in, k, v, kv_in, tail_in, cross_in)

    oq_in = lax.ppermute(oq_out, "dp", partner)

    out_all, dq_all, dkv_own, back_out, cross_out, trade_out = call(
        early_kernel, "early", head + [vmem] * 9 + [anywhere] * 2, [anywhere, anywhere] + [vmem] * 4,
        [
            wide,
            wide,
            made(rows, 2 * key_width, F32),
            made(WINDOW, 2 * key_width),
            made(block_rows, 2 * key_width),
            made(block_rows, 2 * key_width),
        ],
        [pltpu.VMEM((rows + WINDOW, 2 * key_width), BF16), pltpu.VMEM((rows + WINDOW, 2 * key_width), F32)] + tile_scratch,
        6e9, 24, {12: 0, 13: 1},
    )(swap_flags, sinks, docs, q, g, k, v, kv_in, tail_in, cross_in, dkv_late, dkv_swap, out_late, dq_late)

    back_in = lax.ppermute(back_out, "ctx", reverse(forward))
    cross_back = lax.ppermute(cross_out, ("dp", "ctx"), reverse(across))
    trade_in = lax.ppermute(trade_out, "dp", partner)

    final = call(
        finish_kernel, "finish", [smem] + [vmem] * 5 + [anywhere] * 2, [anywhere, anywhere, vmem, vmem],
        [wide, wide, made(rows, key_width), made(rows, key_width)],
        [pltpu.SemaphoreType.DMA((2,))], 1e6, 4, {6: 0, 7: 1},
    )(swap_flags, oq_in, dkv_own, back_in, cross_back, trade_in, out_all, dq_all)
    return tuple(array[None] for array in final)


def solution(mesh):
    blocks = P(("groups", "dp"), "ctx", None)
    in_specs = (blocks, blocks, blocks, blocks, P(), P(("groups", "dp"), None), blocks)
    out_specs = (blocks, blocks, blocks, blocks)
    return jax.shard_map(shards, mesh=mesh, in_specs=in_specs, out_specs=out_specs, check_vma=False)
```
